32 devices in a mesh: rep: 2 (over x), grp: 8 (over z, y), loc: 2 (over core).
Axes of the slice: x: 2, y: 2, z: 4, core: 2. Of those that a mesh axis runs over, the one named last changes fastest.
Arguments:
- tokens: bfloat16 [4096, 3584], P(('rep', 'grp', 'loc')), parts along dimension 0, may hold values from -6 to 6
- norm_gain: float32 [3584], replicated, may hold values from 0.5 to 1.5
- gate_weight: bfloat16 [8, 3584, 1024], P('grp', 'loc'), may hold values from -0.09375 to 0.09375
- up_weight: bfloat16 [8, 3584, 1024], P('grp', 'loc'), may hold values from -0.09375 to 0.09375
- down_weight: bfloat16 [8, 1024, 3584], P('grp', None, 'loc'), may hold values from -0.1875 to 0.1875
- expert_ids: int32 [4096, 4], P(('rep', 'grp', 'loc')), parts along dimension 0, may hold values from 0 to 7, as said below
- numerators: int32 [4096, 4], P(('rep', 'grp', 'loc')), parts along dimension 0, may hold values from 1 to 128
Outputs:
- moe_out: bfloat16 [4096, 3584], P(('rep', 'grp', 'loc')), parts along dimension 0
The draws below stay inside these ranges and needn't reach their ends.
There are 2 independent parts, one for each index of `rep`. The reference program is written for one: setup_inputs(seed, part) draws one part's arguments, and reference() takes and returns one part's arrays. A program takes and returns all parts, laid end to end along the dimension named above; an argument that names none is the same for every part. Nothing has to cross between parts.
Inputs may be any that keep to these rules, and one draw needn't show every extreme that they name: `expert_ids`: expert e lies in group e // 1. Each token names 4 different experts, one in each of four different groups. In each aligned block of 128 tokens every group is named by exactly half of the tokens, no expert is named by more than 64 tokens, and some expert is named by exactly 64; some experts are named by 64 tokens of every block.
All inputs are finite; a program needn't handle non-finite values.
Results may differ from the reference program's by a relative error of at most 0.015.
Values may be sent and summed in bfloat16 or wider, within the bound.
No kernel may reach another device: no remote copies, remote signals or barrier semaphores. Data moves between devices by JAX's collectives and lax.ppermute only.
A program may use at most 64 MiB of HBM per device.

```python
import jax
import jax.numpy as jnp
from jax import lax

D = 3584
FF_WIN = 1024
TOPK = 4
TOK_DEV = 128
EXPERTS = 8
TOKENS = 2048
CAP = 64


def draw_expert_ids(key, part):
    sources = TOKENS // TOK_DEV
    per_group = EXPERTS // 8
    half_tok = TOK_DEV // 2
    hot_member = jax.random.randint(jax.random.fold_in(key, 11), (8,), 0, per_group)
    bounds = jnp.array([9, 17, 25], jnp.int32) * (half_tok // 32)

    def one_source(source_key):
        key_order, key_group, key_offset, key_member = jax.random.split(source_key, 4)
        group_label = jax.random.permutation(key_group, 8)
        token_rank = jax.random.permutation(key_order, TOK_DEV)
        side_index = token_rank // half_tok
        slot_group = group_label[2 * jnp.arange(TOPK)[None, :] + side_index[:, None]]
        offsets = jax.random.randint(key_offset, (TOPK,), 0, half_tok)
        within = (token_rank[:, None] % half_tok + offsets[None, :]) % half_tok
        if per_group > 1:
            member_rank = jnp.sum((within[:, :, None] >= bounds[None, None, :]).astype(jnp.int32), axis=2)
            member_keys = jax.random.split(key_member, 8)
            rest_perm = jax.vmap(lambda member_key: jax.random.permutation(member_key, per_group - 1) + 1)(member_keys)
            shift_table = jnp.concatenate([jnp.zeros((8, 1), jnp.int32), rest_perm.astype(jnp.int32)], axis=1)
            member = (hot_member[slot_group] + shift_table[slot_group, member_rank]) % per_group
        else:
            member = jnp.zeros_like(slot_group)
        return slot_group * per_group + member
    chosen_ids = jax.vmap(one_source)(jax.random.split(jax.random.fold_in(key, 7), sources))
    return chosen_ids.reshape(TOKENS, TOPK).astype(jnp.int32)


def place_ends(values, stream_key, smallest, high):
    dims = values.shape
    place = [jax.random.randint(jax.random.fold_in(stream_key, axis), (), 0, dims[axis]) for axis in range(len(dims))]
    values = values.at[tuple(place)].set(smallest)
    longest = dims.index(max(dims))
    place[longest] = (place[longest] + 1) % dims[longest]
    return values.at[tuple(place)].set(high)


def steps_of(own_key, dims, pieces, smallest, largest):
    def one(position, blocks):
        heights = jax.random.uniform(jax.random.fold_in(jax.random.fold_in(own_key, 6), position), (blocks,), jnp.float32, smallest / len(pieces), largest / len(pieces))
        return jnp.repeat(jnp.exp(heights), dims[position] // blocks).reshape((-1,) + (1,) * (len(dims) - position - 1))

    level = one(*pieces[0])
    for cut in pieces[1:]:
        level = level * one(*cut)
    return level


def bell_draw(rng, dims, spread, limit, shards=(), held_as=jnp.bfloat16):
    result = spread * jax.random.normal(rng, dims, jnp.float32)
    if shards:
        result = result * steps_of(rng, dims, shards, -0.22, 0.18)
    return jnp.clip(result, -limit, limit).astype(held_as)


def setup_inputs(seed: int = 0, part: int = 0) -> dict:
    streams_of = jax.random.split(jax.random.key(seed), 8)
    part_keys = jax.random.split(jax.random.fold_in(streams_of[7], part), 8)
    tokens = bell_draw(part_keys[0], (TOKENS, D), 1.0, 6.0, ((0, 16),))
    norm_gain = jnp.clip(1.0 + 0.1 * jax.random.normal(streams_of[1], (D,), jnp.float32), 0.5, 1.5)
    gate_weight = bell_draw(streams_of[2], (EXPERTS, D, FF_WIN), D ** -0.5, 0.09375, ((0, 8), (1, 2)))
    up_weight = bell_draw(streams_of[3], (EXPERTS, D, FF_WIN), D ** -0.5, 0.09375, ((0, 8), (1, 2)))
    down_weight = bell_draw(streams_of[4], (EXPERTS, FF_WIN, D), FF_WIN ** -0.5, 0.1875, ((0, 8), (2, 2)))
    expert_ids = draw_expert_ids(jax.random.fold_in(jax.random.fold_in(streams_of[7], part), 71), part)
    numerators = place_ends(jax.random.randint(part_keys[6], (TOKENS, TOPK), 1, 129), jax.random.fold_in(part_keys[6], 1), 1, 128).astype(jnp.int32)
    return {"tokens": tokens, "norm_gain": norm_gain, "gate_weight": gate_weight, "up_weight": up_weight, "down_weight": down_weight, "expert_ids": expert_ids, "numerators": numerators}


def rounded(number):
    return lax.optimization_barrier(number.astype(jnp.bfloat16)).astype(jnp.float32)

def expert_rows(rows, w_gate, w_up, w_down):
    half_width = D // 2

    def split_product(weight):
        first_part = jnp.dot(rows[:, :half_width], weight[:half_width], preferred_element_type=jnp.float32)
        second_part = jnp.dot(rows[:, half_width:], weight[half_width:], preferred_element_type=jnp.float32)
        return rounded(first_part) + rounded(second_part)
    gate_sum = split_product(w_gate)
    up_sum = split_product(w_up)
    hidden = (jax.nn.silu(gate_sum) * up_sum).astype(jnp.bfloat16)
    return jnp.dot(hidden, w_down, preferred_element_type=jnp.float32).astype(jnp.bfloat16)

def reference(tokens, norm_gain, gate_weight, up_weight, down_weight, expert_ids, numerators):
    values = tokens.astype(jnp.float32)
    norm_scale = lax.rsqrt(lax.optimization_barrier(jnp.mean(values * values, axis=-1, keepdims=True)) + 1e-06)
    normed = (values * norm_scale * norm_gain.astype(jnp.float32)).astype(jnp.bfloat16)
    sources = TOKENS // TOK_DEV
    pair_ids = expert_ids.reshape(sources, TOK_DEV * TOPK)
    onehot = (pair_ids[:, :, None] == jnp.arange(EXPERTS, dtype=jnp.int32)[None, None, :]).astype(jnp.int32)
    slot_rank = lax.optimization_barrier(jnp.sum((jnp.cumsum(onehot, axis=1) - 1) * onehot, axis=2))
    row_index = (jnp.arange(sources, dtype=jnp.int32)[:, None] * CAP + slot_rank).reshape(-1).astype(jnp.int32)
    token_index = (jnp.arange(TOKENS * TOPK, dtype=jnp.int32) // TOPK).astype(jnp.int32)
    flat_ids = expert_ids.reshape(-1)
    row_table = jnp.full((EXPERTS, sources * CAP), TOKENS, jnp.int32).at[flat_ids, row_index].set(token_index)
    padded = jnp.concatenate([normed, jnp.zeros((1, D), jnp.bfloat16)], axis=0)

    def one_expert(operands):
        rows_of, w_gate, w_up, w_down = operands
        return expert_rows(padded[rows_of], w_gate, w_up, w_down)
    results = lax.map(one_expert, (row_table, gate_weight, up_weight, down_weight))
    picked = results[flat_ids, row_index].astype(jnp.float32).reshape(TOKENS, TOPK, D)
    weights = numerators.astype(jnp.float32) / 128.0
    return lax.optimization_barrier(jnp.sum(picked * weights[:, :, None], axis=1)).astype(jnp.bfloat16)
```

```python
import jax
import jax.numpy as jnp
from jax import lax
from jax.sharding import PartitionSpec as P


def local(tokens, norm_gain, gate_weight, up_weight, down_weight, expert_ids, numerators):
    tok_count, width = tokens.shape
    chosen = expert_ids.shape[1]
    experts = lax.axis_size("grp")
    halves = lax.axis_size("loc")
    half_width = width // halves
    capacity = tok_count // 2 - experts // 32 * (23 * tok_count // 64)
    pair = 2
    length = experts // pair
    order = list(range(0, length, 2)) + list(range(1, length, 2))[::-1]

    def ring(steps):
        return [
            (order[i] * pair + b, order[(i + steps) % length] * pair + b)
            for i in range(length)
            for b in range(pair)
        ]

    swap_pair = [(e, e ^ 1) for e in range(experts)]
    swap_loc = [(0, 1), (1, 0)]
    me = lax.axis_index("grp")
    core = lax.axis_index("loc")

    raw = jnp.concatenate([expert_ids.T, numerators.T], axis=0)
    raw = jnp.stack([raw, lax.ppermute(raw, "loc", swap_loc)])
    raws = [raw] + [lax.ppermute(raw, "grp", ring(s)) for s in range(1, length)]
    raws = jnp.stack(raws)
    ids, nums = raws[:, :, :chosen], raws[:, :, chosen:]
    blocks = jnp.stack([core, 1 - core])
    before = (
        jnp.arange(tok_count)[:, None] < jnp.arange(tok_count)[None, :]
    ).astype(jnp.bfloat16)

    def routes(expert):
        hit = ids == expert
        named = jnp.any(hit, axis=2)
        slot = jnp.einsum(
            "sbt,tu->sbu", named.astype(jnp.bfloat16), before, preferred_element_type=jnp.float32
        ).astype(jnp.int32)
        row = jnp.where(named, blocks[None, :, None] * capacity + slot, -1)
        weight = jnp.sum(jnp.where(hit, nums, 0), axis=2).astype(jnp.float32) / 128.0
        row = row.reshape(length, 1, 2 * tok_count)
        weight = weight.reshape(length, 1, 2 * tok_count)
        at = row == jnp.arange(2 * capacity, dtype=jnp.int32)[None, :, None]
        return at.astype(jnp.bfloat16), jnp.where(at, weight, 0.0).astype(jnp.bfloat16)

    select_own, combine_own = routes(me)
    select_pair, combine_pair = routes(me ^ 1)

    values = tokens.astype(jnp.float32)
    norm_scale = lax.rsqrt(jnp.mean(values * values, axis=-1, keepdims=True) + 1e-06)
    normed = (values * norm_scale * norm_gain).astype(jnp.bfloat16)
    low, high = normed[:, :half_width], normed[:, half_width:]
    mine = jnp.where(core == 0, low, high)
    other = lax.ppermute(jnp.where(core == 0, high, low), "loc", swap_loc)

    def dot(a, b):
        return jnp.dot(a, b, preferred_element_type=jnp.float32)

    def expert(own, brought):
        rows = jnp.concatenate([own, brought], axis=0)
        gate_part = dot(rows, gate_weight[0]).astype(jnp.bfloat16)
        up_part = dot(rows, up_weight[0]).astype(jnp.bfloat16)
        gate_far = lax.ppermute(gate_part, "loc", swap_loc)
        up_far = lax.ppermute(up_part, "loc", swap_loc)
        gate = gate_part.astype(jnp.float32) + gate_far.astype(jnp.float32)
        up = up_part.astype(jnp.float32) + up_far.astype(jnp.float32)
        hidden = (jax.nn.silu(gate) * up).astype(jnp.bfloat16)
        return dot(hidden, down_weight[0]).astype(jnp.bfloat16)

    def mix(weights, rows):
        return jnp.einsum("rk,rf->kf", weights, rows, preferred_element_type=jnp.float32)

    def contribution(s, chunk):
        own = dot(select_own[s], chunk).astype(jnp.bfloat16)
        leaving = dot(select_pair[s], chunk).astype(jnp.bfloat16)
        brought = lax.ppermute(leaving, "grp", swap_pair)
        out = expert(own, brought)
        back = lax.ppermute(out[2 * capacity :], "grp", swap_pair)
        return mix(combine_own[s], out[: 2 * capacity]) + mix(combine_pair[s], back)

    held = [(mine, other)]
    for _ in range(1, length):
        held.append(tuple(lax.ppermute(half, "grp", ring(1)) for half in held[-1]))
    parts = [contribution(s, jnp.concatenate(held[s], axis=0)) for s in range(length)]
    mine_sum, other_sum = 0.0, 0.0
    for s in range(1, length):
        other_sum = lax.ppermute(
            (parts[s][tok_count:] + other_sum).astype(jnp.bfloat16), "grp", ring(1)
        ).astype(jnp.float32)
        mine_sum = lax.ppermute(
            (parts[s][:tok_count] + mine_sum).astype(jnp.bfloat16), "grp", ring(1)
        ).astype(jnp.float32)
    other_sum = (parts[0][tok_count:] + other_sum).astype(jnp.bfloat16)
    mine_sum = (parts[0][:tok_count] + mine_sum).astype(jnp.bfloat16)
    brought = lax.ppermute(other_sum, "loc", swap_loc)
    low = jnp.where(core == 0, mine_sum, brought)
    high = jnp.where(core == 0, brought, mine_sum)
    return jnp.concatenate([low, high], axis=1)


def solution(mesh):
    in_specs = (
        P(("rep", "grp", "loc"), None),
        P(),
        P("grp", "loc", None),
        P("grp", "loc", None),
        P("grp", None, "loc"),
        P(("rep", "grp", "loc"), None),
        P(("rep", "grp", "loc"), None),
    )
    out_specs = P(("rep", "grp", "loc"), None)
    return jax.shard_map(local, mesh=mesh, in_specs=in_specs, out_specs=out_specs, check_vma=False)
```
